32 devices in a mesh: groups: 2 (over y), tile: 8 (over z, x), head: 2 (over core).
Axes of the slice: x: 2, y: 2, z: 4, core: 2. Of those that a mesh axis runs over, the one named last changes fastest.
Arguments:
- tissue_tiles: bfloat16 [128, 32, 32, 128], P(('groups', 'tile', 'head')), parts along dimension 0, may hold values from -64 to 64
- neighbours: int32 [128, 8], P(('groups', 'tile', 'head')), parts along dimension 0, may hold values from -1 to 63, as said below
- conv_weight: bfloat16 [3, 3, 128, 128], replicated, may hold values from -0.1875 to 0.1875
- conv_bias: float32 [128], replicated, may hold values from -2 to 2
- head_weight: float32 [128], replicated, may hold values from -3 to 3
- slide_label: int32 [2], P('groups'), parts along dimension 0, may hold values from 0 to 100
Outputs:
- grad_tiles: float32 [128, 32, 32, 128], P(('groups', 'tile', 'head')), parts along dimension 0
The draws below stay inside these ranges and needn't reach their ends.
There are 2 independent parts, one for each index of `groups`. The reference program is written for one: setup_inputs(seed, part) draws one part's arguments, and reference() takes and returns one part's arrays. A program takes and returns all parts, laid end to end along the dimension named above; an argument that names none is the same for every part. Nothing has to cross between parts.
Inputs may be any that keep to these rules, and one draw needn't show every extreme that they name: `neighbours`: tiles are listed row by row of a strip of the slide 3 tiles wide in which background cells are left out; entry k of a tile is its neighbour in direction k or -1 where that cell is background or outside the strip. Neighbour relations are mutual.
All inputs are finite; a program needn't handle non-finite values.
Results may differ from the reference program's by a relative error of at most 0.0029.
Values may be sent and summed in bfloat16 or wider, within the bound.
No kernel may reach another device: no remote copies, remote signals or barrier semaphores. Data moves between devices by JAX's collectives and lax.ppermute only.
A program may use at most 64 MiB of HBM per device.

```python
import math
import jax
import jax.numpy as jnp
from jax import lax

C = 128
S = 32
DILATION_STEP = 2
GW = 3
TILES = 64


def draw_neighbours(key, part):
    skipped = (jax.random.randint(jax.random.fold_in(key, 11), (TILES,), 0, 4) == 0).astype(jnp.int32)
    cell_index = jnp.arange(TILES, dtype=jnp.int32) + jnp.cumsum(skipped).astype(jnp.int32)
    column_index = cell_index % GW
    listed = []
    for row_step, col_step in ((-1, -1), (-1, 0), (-1, 1), (0, -1), (0, 1), (1, -1), (1, 0), (1, 1)):
        target_cell = cell_index + row_step * GW + col_step
        inside = (column_index + col_step >= 0) & (column_index + col_step < GW)
        position = jnp.clip(jnp.searchsorted(cell_index, target_cell), 0, TILES - 1).astype(jnp.int32)
        present = inside & (cell_index[position] == target_cell)
        listed.append(jnp.where(present, position, -1).astype(jnp.int32))
    return jnp.stack(listed, 1)


def draw_tissue_tiles(key, part):
    tile_pos = jnp.arange(TILES, dtype=jnp.float32) / max(TILES - 1, 1)
    jitter = jax.random.uniform(jax.random.fold_in(key, 21), (TILES,), minval=-0.35, maxval=0.35)
    tile_scale = 0.5 * jnp.exp(tile_pos * math.log(6.0)) * jnp.exp(jitter)
    chan_scale = jnp.exp(jax.random.uniform(jax.random.fold_in(key, 22), (C,), minval=math.log(0.5), maxval=math.log(2.0)))
    tile_ids = jnp.arange(TILES, dtype=jnp.int32)
    region_shift = jax.random.randint(jax.random.fold_in(key, 25), (), 0, TILES).astype(jnp.int32)
    region = ((tile_ids + region_shift) % TILES * 4 // TILES).astype(jnp.int32)
    patterns = 6.0 * jnp.clip(jax.random.normal(jax.random.fold_in(key, 26), (4, C), jnp.float32), -3.0, 3.0)
    tile_amp = jax.random.uniform(jax.random.fold_in(key, 27), (TILES,), minval=0.6, maxval=1.4)
    pixel_pos = (jnp.arange(S, dtype=jnp.float32) + 0.5) * (math.pi / S)
    bump = jnp.sin(pixel_pos)[:, None] * jnp.sin(pixel_pos)[None, :]
    region_part = tile_amp[:, None] * patterns[region]
    offset = region_part[:, None, None, :] * bump[None, :, :, None]
    values = jnp.clip(jax.random.normal(jax.random.fold_in(key, 23), (TILES, S, S, C), jnp.float32), -3.0, 3.0)
    return (values * tile_scale[:, None, None, None] * chan_scale + offset).astype(jnp.bfloat16)


def centred(rng, extent, scale, most, held_as=jnp.bfloat16):
    return jnp.clip(scale * jax.random.normal(rng, extent, jnp.float32), -most, most).astype(held_as)


def setup_inputs(seed: int = 0, part: int = 0) -> dict:
    arg_keys = jax.random.split(jax.random.key(seed), 7)
    own_keys = jax.random.split(jax.random.fold_in(arg_keys[6], part), 7)
    return {
        "tissue_tiles": draw_tissue_tiles(jax.random.fold_in(jax.random.fold_in(arg_keys[6], part), 71), part),
        "neighbours": draw_neighbours(jax.random.fold_in(jax.random.fold_in(arg_keys[6], part), 71), part),
        "conv_weight": centred(arg_keys[2], (3, 3, C, C), (9 * C) ** -0.5, 0.1875),
        "conv_bias": centred(arg_keys[3], (C,), 0.5, 2.0, jnp.float32),
        "head_weight": centred(arg_keys[4], (C,), 1.0, 3.0, jnp.float32),
        "slide_label": jax.random.randint(own_keys[5], (1,), 0, 101).astype(jnp.int32),
    }


def extend(tile_feature_maps, neighbours):
    tile_count = tile_feature_maps.shape[0]
    side_length = tile_feature_maps.shape[1]
    blank = jnp.zeros((1,) + tile_feature_maps.shape[1:], tile_feature_maps.dtype)
    widened_maps = jnp.concatenate([tile_feature_maps, blank], 0)
    index_list = jnp.where(neighbours < 0, tile_count, neighbours).astype(jnp.int32)
    upper_margin = widened_maps[:, :DILATION_STEP]
    lower_margin = widened_maps[:, side_length - DILATION_STEP:]
    left_margin = widened_maps[:, :, :DILATION_STEP]
    right_margin = widened_maps[:, :, side_length - DILATION_STEP:]

    def gather_band(strips, direction):
        return jnp.take(strips, index_list[:, direction], axis=0)

    rows_above_tile = jnp.concatenate([gather_band(lower_margin, 0)[:, :, side_length - DILATION_STEP:], gather_band(lower_margin, 1), gather_band(lower_margin, 2)[:, :, :DILATION_STEP]], 2)
    middle_rows = jnp.concatenate([gather_band(right_margin, 3), tile_feature_maps, gather_band(left_margin, 4)], 2)
    rows_below_tile = jnp.concatenate([gather_band(upper_margin, 5)[:, :, side_length - DILATION_STEP:], gather_band(upper_margin, 6), gather_band(upper_margin, 7)[:, :, :DILATION_STEP]], 2)
    return jnp.concatenate([rows_above_tile, middle_rows, rows_below_tile], 1)


def dilated(padded_maps, kernel_weight):
    return lax.conv_general_dilated(padded_maps.astype(jnp.float32), kernel_weight.astype(jnp.float32), (1, 1), "VALID", rhs_dilation=(DILATION_STEP, DILATION_STEP), dimension_numbers=("NHWC", "HWIO", "NHWC"), precision=lax.Precision.HIGHEST)


def reference(tissue_tiles, neighbours, conv_weight, conv_bias, head_weight, slide_label):
    padded_maps = extend(tissue_tiles, neighbours)
    pre = dilated(padded_maps, conv_weight) + conv_bias
    sigmoid_pre = jax.nn.sigmoid(pre)
    slide_score = jnp.sum(pre * sigmoid_pre * head_weight) / (TILES * S * S * C)
    loss_slope = jax.nn.sigmoid(slide_score) - slide_label[0].astype(jnp.float32) / 100.0
    grad_pre = (loss_slope * head_weight * sigmoid_pre * (1.0 + pre * (1.0 - sigmoid_pre))).astype(jnp.bfloat16)
    grad_padded = extend(grad_pre, neighbours)
    flipped = jnp.transpose(conv_weight[::-1, ::-1], (0, 1, 3, 2))
    return dilated(grad_padded, flipped)
```

```python
import functools

import jax
import jax.numpy as jnp
from jax import lax
from jax.experimental import pallas as pl
from jax.experimental.pallas import tpu as pltpu
from jax.sharding import PartitionSpec as P

D = 2
GROUP = ("tile", "head")
BF = jnp.bfloat16
F32 = jnp.float32
VMEM = pl.BlockSpec(memory_space=pltpu.VMEM)
SMEM = pl.BlockSpec(memory_space=pltpu.SMEM)


def strips_kernel(top_ref, bottom_ref, left_ref, right_ref, up_ref, down_ref):
    t = top_ref.shape[0]
    s = left_ref.shape[1]
    up_ref[0:t] = top_ref[...]
    down_ref[0:t] = bottom_ref[...]
    per = up_ref.shape[2] // D
    for i in range(s):
        at = pl.ds((i % per) * D, D)
        up_ref[t, i // per, at, :] = left_ref[0, i, 0:D, :]
        down_ref[t, i // per, at, :] = right_ref[0, i, right_ref.shape[2] - D :, :]


def make_strips(maps):
    t, s, _, c = maps.shape
    edge = 16
    out = jax.ShapeDtypeStruct((t + 1, D, s, c), maps.dtype)
    return pl.pallas_call(
        strips_kernel,
        grid=(1,),
        out_shape=(out, out),
        in_specs=[
            pl.BlockSpec((t, D, s, c), lambda i: (0, 0, 0, 0)),
            pl.BlockSpec((t, D, s, c), lambda i: (0, s // D - 1, 0, 0)),
            pl.BlockSpec((1, s, edge, c), lambda i: (0, 0, 0, 0)),
            pl.BlockSpec((1, s, edge, c), lambda i: (t - 1, 0, s // edge - 1, 0)),
        ],
        out_specs=(pl.BlockSpec(out.shape, lambda i: (0, 0, 0, 0)),) * 2,
        name="strips",
    )(maps, maps, maps, maps)


def exchange(up, down):
    size = lax.axis_size(GROUP)
    forward = [(i, i + 1) for i in range(size - 1)]
    return (
        lax.ppermute(down, GROUP, forward),
        lax.ppermute(up, GROUP, [(j, i) for i, j in forward]),
    )


def weights_kernel(w_ref, first_ref, second_ref):
    c = w_ref.shape[2]
    blank = jnp.zeros((c, c), BF)
    for b in range(3):
        for m in range(4):
            rows = pl.ds((m * 3 + b) * c, c)
            for half in range(2):
                a = m - half
                cols = pl.ds(half * c, c)
                if 0 <= a < 3:
                    first_ref[rows, cols] = w_ref[a, b]
                    second_ref[rows, cols] = w_ref[2 - a, 2 - b].T
                else:
                    first_ref[rows, cols] = blank
                    second_ref[rows, cols] = blank


def make_weights(w):
    c = w.shape[2]
    out = jax.ShapeDtypeStruct((12 * c, 2 * c), BF)
    return pl.pallas_call(
        weights_kernel,
        out_shape=(out, out),
        in_specs=[VMEM],
        out_specs=(VMEM, VMEM),
        cost_estimate=pl.CostEstimate(flops=0, bytes_accessed=2 << 20, transcendentals=0),
        name="weights",
    )(w)


def fill_window(near_ref, start_ref, src_ref, prev_ref, next_ref, win_ref, low_ref, high_ref):
    t, s, _, c = src_ref.shape
    start = start_ref[0]
    low_ref[0:t] = prev_ref[0:t]
    low_ref[t : 2 * t] = src_ref[:, s - D :]
    low_ref[2 * t] = jnp.zeros(low_ref.shape[1:], BF)
    high_ref[0:t] = src_ref[:, 0:D]
    high_ref[t : 2 * t] = next_ref[0:t]
    high_ref[2 * t] = jnp.zeros(low_ref.shape[1:], BF)

    def pick(ref, tile, k, base):
        there = near_ref[tile, k]
        local = jnp.where(there < 0, 2 * t, jnp.clip(there - base, 0, 2 * t - 1))
        return ref[local]

    per = s // D
    for i in range(t):
        v = src_ref[i]
        win_ref[0, i, D : D + s, D:] = v[:, : s - D]
        win_ref[1, i, D : D + s] = v
        win_ref[2, i, D : D + s, : s - D] = v[:, D:]
        has_left = (near_ref[i, 3] >= 0).astype(F32).astype(BF)
        has_right = (near_ref[i, 4] >= 0).astype(F32).astype(BF)
        if i > 0:
            win_ref[0, i, D : D + s, :D] = src_ref[i - 1, :, s - D :] * has_left
        else:
            for r in range(s):
                win_ref[0, i, D + r, :D] = (
                    prev_ref[t, r // per, pl.ds((r % per) * D, D), :] * has_left
                )
        if i < t - 1:
            win_ref[2, i, D : D + s, s - D :] = src_ref[i + 1, :, :D] * has_right
        else:
            for r in range(s):
                win_ref[2, i, D + r, s - D :] = (
                    next_ref[t, r // per, pl.ds((r % per) * D, D), :] * has_right
                )
        for ref, k, base, row in ((low_ref, 0, start - t, 0), (high_ref, 5, start, D + s)):
            rows = slice(row, row + D)
            middle = pick(ref, i, k + 1, base)
            win_ref[0, i, rows, D:] = middle[:, : s - D]
            win_ref[0, i, rows, :D] = pick(ref, i, k, base)[:, s - D :]
            win_ref[1, i, rows] = middle
            win_ref[2, i, rows, : s - D] = middle[:, D:]
            win_ref[2, i, rows, s - D :] = pick(ref, i, k + 2, base)[:, :D]


def band(win_ref, tile, group, groups):
    s, c = win_ref.shape[3:]
    pieces = []
    for m in range(4):
        for b in range(3):
            pair = [
                win_ref[b, tile, pl.ds(4 * g + D * m, D)]
                for g in range(group, group + groups)
            ]
            pieces.append(jnp.concatenate(pair, 0).reshape(groups * D * s, c))
    return jnp.concatenate(pieces, 1)


def first_kernel(
    groups, near_ref, start_ref, x_ref, prev_ref, next_ref, w_ref, bias_ref, head_ref,
    u_ref, up_ref, down_ref, sum_ref, win_ref, low_ref, high_ref,
):
    fill_window(near_ref, start_ref, x_ref, prev_ref, next_ref, win_ref, low_ref, high_ref)
    t, s, _, c = x_ref.shape
    bias = bias_ref[...]
    head = head_ref[...]
    total = jnp.zeros((8, c), F32)
    for tile in range(t):
        for group in range(0, s // 4, groups):
            both = jnp.dot(
                band(win_ref, tile, group, groups), w_ref[...], preferred_element_type=F32
            )
            for half in range(2):
                pre = both[:, half * c : (half + 1) * c] + bias
                sig = 0.5 + 0.5 * jnp.tanh(0.5 * pre)
                silu = pre * sig
                total = total + jnp.sum(silu.reshape(-1, 8, c), 0)
                grad = (head * (sig + silu * (1.0 - sig))).astype(BF)
                grad = grad.reshape(groups, D, s, c)
                for g in range(groups):
                    u_ref[tile, pl.ds(4 * (group + g) + D * half, D)] = grad[g]
    sum_ref[...] = total * head
    per = s // D
    up_ref[0:t] = u_ref[:, 0:D]
    down_ref[0:t] = u_ref[:, s - D :]
    for i in range(s):
        at = pl.ds((i % per) * D, D)
        up_ref[t, i // per, at, :] = u_ref[0, i, 0:D, :]
        down_ref[t, i // per, at, :] = u_ref[t - 1, i, s - D :, :]


def window_scratch(t, s, c):
    return [
        pltpu.VMEM((3, t, s + 2 * D, s, c), BF),
        pltpu.VMEM((2 * t + 1, D, s, c), BF),
        pltpu.VMEM((2 * t + 1, D, s, c), BF),
    ]


def first_stage(near, start, x, before, after, w, bias, head, groups=8):
    t, s, _, c = x.shape
    strip = jax.ShapeDtypeStruct((t + 1, D, s, c), BF)
    return pl.pallas_call(
        functools.partial(first_kernel, groups),
        out_shape=(
            jax.ShapeDtypeStruct(x.shape, BF),
            strip,
            strip,
            jax.ShapeDtypeStruct((8, c), F32),
        ),
        in_specs=[SMEM, SMEM] + [VMEM] * 6,
        out_specs=(VMEM,) * 4,
        scratch_shapes=window_scratch(t, s, c),
        cost_estimate=pl.CostEstimate(
            flops=2 * 9 * t * s * s * c * c, bytes_accessed=4 << 20, transcendentals=t * s * s * c
        ),
        name="first",
    )(near, start, x, before, after, w, bias, head)


def second_kernel(
    groups, near_ref, start_ref, u_ref, prev_ref, next_ref, w_ref, o_ref, win_ref, low_ref, high_ref
):
    fill_window(near_ref, start_ref, u_ref, prev_ref, next_ref, win_ref, low_ref, high_ref)
    t, s, _, c = u_ref.shape
    for tile in range(t):
        for group in range(0, s // 4, groups):
            both = jnp.dot(
                band(win_ref, tile, group, groups), w_ref[...], preferred_element_type=F32
            )
            for half in range(2):
                part = both[:, half * c : (half + 1) * c].reshape(groups, D, s, c)
                for g in range(groups):
                    o_ref[tile, pl.ds(4 * (group + g) + D * half, D)] = part[g]


def second_stage(near, start, u, before, after, w, groups=8):
    t, s, _, c = u.shape
    return pl.pallas_call(
        functools.partial(second_kernel, groups),
        out_shape=jax.ShapeDtypeStruct(u.shape, F32),
        in_specs=[SMEM, SMEM] + [VMEM] * 4,
        out_specs=VMEM,
        scratch_shapes=window_scratch(t, s, c),
        cost_estimate=pl.CostEstimate(
            flops=2 * 9 * t * s * s * c * c, bytes_accessed=4 << 20, transcendentals=0
        ),
        name="second",
    )(near, start, u, before, after, w)


def scale_kernel(count, label_ref, sum_ref, v_ref, o_ref):
    score = jnp.sum(sum_ref[...], axis=(0, 1), keepdims=True) / count
    label = label_ref[0].astype(F32) / 100.0
    slope = jax.nn.sigmoid(score) - label
    o_ref[...] = v_ref[...] * slope.reshape(1, 1, 1, 1)


def scale(label, total, v, count):
    t, s, _, c = v.shape
    rows = 8
    block = pl.BlockSpec((1, rows, s, c), lambda i, j: (i, j, 0, 0))
    return pl.pallas_call(
        functools.partial(scale_kernel, count),
        grid=(t, s // rows),
        out_shape=jax.ShapeDtypeStruct(v.shape, F32),
        in_specs=[SMEM, pl.BlockSpec(total.shape, lambda i, j: (0, 0)), block],
        out_specs=block,
        name="scale",
    )(label, total, v)


def group_sum(part):
    size = lax.axis_size(GROUP)
    if size & (size - 1):
        return lax.psum(part, GROUP)
    step = 1
    while step < size:
        part = part + lax.ppermute(part, GROUP, [(i, i ^ step) for i in range(size)])
        step *= 2
    return part


def body(tissue_tiles, neighbours, conv_weight, conv_bias, head_weight, slide_label):
    t, s, _, c = tissue_tiles.shape
    start = (lax.axis_index(GROUP) * t).astype(jnp.int32).reshape(1)
    before, after = exchange(*make_strips(tissue_tiles))
    w_first, w_second = make_weights(conv_weight)
    u, up, down, part = first_stage(
        neighbours, start, tissue_tiles, before, after, w_first,
        conv_bias.reshape(1, c), head_weight.reshape(1, c),
    )
    total = group_sum(part)
    before, after = exchange(up, down)
    v = second_stage(neighbours, start, u, before, after, w_second)
    return scale(slide_label, total, v, float(t * lax.axis_size(GROUP) * s * s * c))


def solution(mesh):
    return jax.shard_map(
        body,
        mesh=mesh,
        in_specs=(
            P(("groups", "tile", "head"), None, None, None),
            P(("groups", "tile", "head"), None),
            P(),
            P(),
            P(),
            P("groups"),
        ),
        out_specs=P(("groups", "tile", "head"), None, None, None),
        check_vma=False,
    )
```

```python
import functools

import jax
import jax.numpy as jnp
from jax import lax
from jax.experimental import pallas as pl
from jax.experimental.pallas import tpu as pltpu
from jax.sharding import PartitionSpec as P

D = 2
GROUP = ("tile", "head")
BF = jnp.bfloat16
F32 = jnp.float32
VMEM = pl.BlockSpec(memory_space=pltpu.VMEM)
SMEM = pl.BlockSpec(memory_space=pltpu.SMEM)


LIMIT = 24 << 20


def params(limit=LIMIT):
    return pltpu.CompilerParams(vmem_limit_bytes=limit)


def put_strips(parity, src_ref, mate_ref, other_ref):
    t, s, _, c = src_ref.shape
    per = s // D

    def put(ref, last):
        ref[0:t] = src_ref[:, s - D :] if last else src_ref[:, 0:D]
        for i in range(s):
            at = pl.ds((i % per) * D, D)
            ref[t, i // per, at, :] = (
                src_ref[t - 1, i, s - D :, :] if last else src_ref[0, i, 0:D, :]
            )

    @pl.when(parity == 0)
    def _():
        put(mate_ref, True)
        put(other_ref, False)

    @pl.when(parity == 1)
    def _():
        put(mate_ref, False)
        put(other_ref, True)


def strips_kernel(place_ref, x_ref, mate_ref, other_ref, keep_ref):
    keep_ref[...] = x_ref[...]
    put_strips(place_ref[1], x_ref, mate_ref, other_ref)


def make_strips(place, x):
    t, s, _, c = x.shape
    out = jax.ShapeDtypeStruct((t + 1, D, s, c), BF)
    return pl.pallas_call(
        strips_kernel,
        out_shape=(out, out, jax.ShapeDtypeStruct(x.shape, BF)),
        in_specs=[SMEM, VMEM],
        out_specs=(VMEM,) * 3,
        compiler_params=params(),
        name="strips",
    )(place, x)


def swap(mate, other):
    size = lax.axis_size(GROUP)
    mates = [(i, i ^ 1) for i in range(size) if i ^ 1 < size]
    others = [(i, j) for i in range(size) for j in [(i + 1 ^ 1) - 1] if 0 <= j < size]
    return lax.ppermute(mate, GROUP, mates), lax.ppermute(other, GROUP, others)


def weights_kernel(w_ref, head_ref, first_ref, second_ref):
    c = w_ref.shape[2]
    blank = jnp.zeros((c, c), BF)
    head = head_ref[...]
    for b in range(3):
        for m in range(4):
            rows = pl.ds((m * 3 + b) * c, c)
            for half in range(2):
                a = m - half
                first_ref[rows, pl.ds(half * c, c)] = w_ref[a, b] if 0 <= a < 3 else blank
        for a in range(3):
            rows = pl.ds((a * 3 + b) * c, c)
            turned = (w_ref[2 - a, 2 - b].astype(F32) * head).T
            high = turned.astype(BF)
            second_ref[rows, 0:c] = high
            second_ref[rows, c : 2 * c] = (turned - high.astype(F32)).astype(BF)


def make_weights(w, head):
    c = w.shape[2]
    return pl.pallas_call(
        weights_kernel,
        out_shape=(
            jax.ShapeDtypeStruct((12 * c, 2 * c), BF),
            jax.ShapeDtypeStruct((9 * c, 2 * c), BF),
        ),
        in_specs=[VMEM, VMEM],
        out_specs=(VMEM, VMEM),
        compiler_params=params(),
        cost_estimate=pl.CostEstimate(flops=0, bytes_accessed=4 << 20, transcendentals=0),
        name="weights",
    )(w, head)


def fill_window(tiles, near_ref, place_ref, src_ref, mate_ref, other_ref, win_ref, strip_ref):
    t, s, _, c = src_ref.shape
    start, parity = place_ref[0], place_ref[1]
    strip_ref[0 : t + 1] = mate_ref[0 : t + 1]
    strip_ref[t + 1 : 2 * t + 2] = other_ref[0 : t + 1]
    strip_ref[2 * t + 2 : 3 * t + 2] = src_ref[:, s - D :]
    strip_ref[3 * t + 2 : 4 * t + 2] = src_ref[:, 0:D]
    strip_ref[4 * t + 2] = jnp.zeros((D, s, c), BF)
    before = (1 - parity) * (t + 1)
    after = parity * (t + 1)

    def pick(tile, k):
        there = near_ref[tile, k]
        local = there - start
        if k < 3:
            local = jnp.clip(local, -t, t - 1)
            slot = jnp.where(local < 0, before + t + local, 2 * t + 2 + local)
        else:
            local = jnp.clip(local, 0, 2 * t - 1)
            slot = jnp.where(local >= t, after - t + local, 3 * t + 2 + local)
        return strip_ref[jnp.where(there < 0, 4 * t + 2, slot)]

    per = s // D
    for j, i in enumerate(tiles):
        v = src_ref[i]
        win_ref[0, j, D : D + s, D:] = v[:, : s - D]
        win_ref[1, j, D : D + s] = v
        win_ref[2, j, D : D + s, : s - D] = v[:, D:]
        has_left = (near_ref[i, 3] >= 0).astype(F32).astype(BF)
        has_right = (near_ref[i, 4] >= 0).astype(F32).astype(BF)
        if i > 0:
            win_ref[0, j, D : D + s, :D] = src_ref[i - 1, :, s - D :] * has_left
        else:
            for r in range(s):
                at = pl.ds((r % per) * D, D)
                win_ref[0, j, D + r, :D] = strip_ref[before + t, r // per, at, :] * has_left
        if i < t - 1:
            win_ref[2, j, D : D + s, s - D :] = src_ref[i + 1, :, :D] * has_right
        else:
            for r in range(s):
                at = pl.ds((r % per) * D, D)
                win_ref[2, j, D + r, s - D :] = strip_ref[after + t, r // per, at, :] * has_right
        for k, row in ((0, 0), (5, D + s)):
            rows = slice(row, row + D)
            middle = pick(i, k + 1)
            win_ref[0, j, rows, D:] = middle[:, : s - D]
            win_ref[0, j, rows, :D] = pick(i, k)[:, s - D :]
            win_ref[1, j, rows] = middle
            win_ref[2, j, rows, : s - D] = middle[:, D:]
            win_ref[2, j, rows, s - D :] = pick(i, k + 2)[:, :D]


def window_scratch(n, t, s, c):
    return [
        pltpu.VMEM((3, n, s + 2 * D, s, c), BF),
        pltpu.VMEM((4 * t + 3, D, s, c), BF),
    ]


def band(win_ref, tile, group, groups):
    s, c = win_ref.shape[3:]
    pieces = []
    for m in range(4):
        for b in range(3):
            pair = [
                win_ref[b, tile, pl.ds(4 * g + D * m, D)]
                for g in range(group, group + groups)
            ]
            pieces.append(jnp.concatenate(pair, 0).reshape(groups * D * s, c))
    return jnp.concatenate(pieces, 1)


def first_kernel(
    groups, near_ref, place_ref, x_ref, mate_ref, other_ref, w_ref, bias_ref, head_ref,
    u_ref, to_mate_ref, to_other_ref, sum_ref, win_ref, strip_ref,
):
    t, s, _, c = x_ref.shape
    fill_window(
        range(t), near_ref, place_ref, x_ref, mate_ref, other_ref, win_ref, strip_ref
    )
    bias = bias_ref[...]
    total = jnp.zeros((16, c), F32)
    for tile in range(t):
        for group in range(0, s // 4, groups):
            both = jnp.dot(
                band(win_ref, tile, group, groups), w_ref[...], preferred_element_type=F32
            )
            for half in range(2):
                pre = both[:, half * c : (half + 1) * c] + bias
                sig = 0.5 + 0.5 * jnp.tanh(0.5 * pre)
                silu = pre * sig
                total = total + jnp.sum(silu.reshape(-1, 16, c), 0)
                grad = (sig + silu * (1.0 - sig)).astype(BF)
                grad = grad.reshape(groups, D, s, c)
                for g in range(groups):
                    u_ref[tile, pl.ds(4 * (group + g) + D * half, D)] = grad[g]
    total = total * head_ref[...]
    sum_ref[...] = total
    put_strips(place_ref[1], u_ref, to_mate_ref, to_other_ref)
    high = total.astype(BF)
    rest = total - high.astype(F32)
    middle = rest.astype(BF)
    to_mate_ref[t + 1, 0, 0:16] = high
    to_mate_ref[t + 1, 0, 16:32] = middle
    to_mate_ref[t + 1, 1, 0:16] = (rest - middle.astype(F32)).astype(BF)
    to_mate_ref[t + 1, 1, 16:32] = jnp.zeros((16, c), BF)


def first_stage(near, place, x, mate, other, w, bias, head, groups=8):
    t, s, _, c = x.shape
    return pl.pallas_call(
        functools.partial(first_kernel, groups),
        out_shape=(
            jax.ShapeDtypeStruct(x.shape, BF),
            jax.ShapeDtypeStruct((t + 2, D, s, c), BF),
            jax.ShapeDtypeStruct((t + 1, D, s, c), BF),
            jax.ShapeDtypeStruct((16, c), F32),
        ),
        in_specs=[SMEM, SMEM] + [VMEM] * 6,
        out_specs=(VMEM,) * 4,
        scratch_shapes=window_scratch(t, t, s, c),
        compiler_params=params(),
        cost_estimate=pl.CostEstimate(
            flops=2 * 9 * t * s * s * c * c, bytes_accessed=4 << 20, transcendentals=t * s * s * c
        ),
        name="first",
    )(near, place, x, mate, other, w, bias, head)


def second_kernel(
    tiles, near_ref, place_ref, u_ref, mate_ref, other_ref, w_ref, o_ref, win_ref, strip_ref
):
    t, s, _, c = u_ref.shape
    fill_window(tiles, near_ref, place_ref, u_ref, mate_ref, other_ref, win_ref, strip_ref)
    for j in range(len(tiles)):
        taken = jnp.concatenate(
            [
                win_ref[b, j, D * a : D * a + s].reshape(s * s, c)
                for a in range(3)
                for b in range(3)
            ],
            1,
        )
        both = jnp.dot(taken, w_ref[...], preferred_element_type=F32)
        o_ref[j] = (both[:, :c] + both[:, c:]).reshape(s, s, c)


def second_stage(tiles, near, place, u, mate, other, w):
    t, s, _, c = u.shape
    n = len(tiles)
    return pl.pallas_call(
        functools.partial(second_kernel, tiles),
        out_shape=jax.ShapeDtypeStruct((n, s, s, c), F32),
        in_specs=[SMEM, SMEM] + [VMEM] * 4,
        out_specs=VMEM,
        scratch_shapes=window_scratch(n, t, s, c),
        compiler_params=params(),
        cost_estimate=pl.CostEstimate(
            flops=2 * 9 * n * s * s * c * c, bytes_accessed=n << 21, transcendentals=0
        ),
        name="second",
    )(near, place, u, mate, other, w)


def scale_kernel(count, n, label_ref, mine_ref, theirs_ref, *refs):
    parts, o_ref, stage_ref, sems = refs[:n], *refs[n:]
    score = jnp.sum(mine_ref[...] + theirs_ref[...], axis=(0, 1), keepdims=True) / count
    slope = jax.nn.sigmoid(score) - label_ref[0].astype(F32) / 100.0
    copies = []
    at = 0
    half = parts[0].shape[1] // 2
    for part in parts:
        for i in range(part.shape[0]):
            for h in range(2):
                rows = pl.ds(h * half, half)
                stage_ref[at, rows] = part[i, rows] * slope.reshape(1, 1, 1)
                copy = pltpu.make_async_copy(
                    stage_ref.at[at, rows], o_ref.at[at, rows], sems.at[at, h]
                )
                copy.start()
                copies.append(copy)
            at += 1
    for copy in copies:
        copy.wait()


def scale(label, mine, theirs, parts, count):
    t = sum(p.shape[0] for p in parts)
    s, _, c = parts[0].shape[1:]
    return pl.pallas_call(
        functools.partial(scale_kernel, count, len(parts)),
        out_shape=jax.ShapeDtypeStruct((t, s, s, c), F32),
        in_specs=[SMEM] + [VMEM] * (2 + len(parts)),
        out_specs=pl.BlockSpec(memory_space=pl.ANY),
        scratch_shapes=[pltpu.VMEM((t, s, s, c), F32), pltpu.SemaphoreType.DMA((t, 2))],
        compiler_params=params(),
        name="scale",
    )(label, mine, theirs, *parts)


def pieces(t):
    return [tuple(range(i, i + 1)) for i in range(t)]


def body(tissue_tiles, neighbours, conv_weight, conv_bias, head_weight, slide_label):
    t, s, _, c = tissue_tiles.shape
    size = lax.axis_size(GROUP)
    index = lax.axis_index(GROUP).astype(jnp.int32)
    place = jnp.stack([index * t, index % 2])
    head = head_weight.reshape(1, c)
    mate, other, x = make_strips(place, tissue_tiles)
    mate, other = swap(mate, other)
    w_first, w_second = make_weights(conv_weight, head)
    u, mate, other, mine = first_stage(
        neighbours, place, x, mate, other, w_first, conv_bias.reshape(1, c), head
    )
    mate, other = swap(mate, other)
    got = mate[t + 1].astype(F32)
    theirs = got[0, 0:16] + got[0, 16:32] + got[1, 0:16]
    if size & (size - 1):
        mine, theirs = lax.psum(mine, GROUP), jnp.zeros_like(mine)
    step = 2
    while step < size and not size & (size - 1):
        mine = mine + theirs
        theirs = lax.ppermute(mine, GROUP, [(i, i ^ step) for i in range(size)])
        step *= 2
    parts = [
        second_stage(tiles, neighbours, place, u, mate, other, w_second) for tiles in pieces(t)
    ]
    return scale(slide_label, mine, theirs, parts, float(t * size * s * s * c))


def solution(mesh):
    return jax.shard_map(
        body,
        mesh=mesh,
        in_specs=(
            P(("groups", "tile", "head"), None, None, None),
            P(("groups", "tile", "head"), None),
            P(),
            P(),
            P(),
            P("groups"),
        ),
        out_specs=P(("groups", "tile", "head"), None, None, None),
        check_vma=False,
    )
```

```python
import functools

import jax
import jax.numpy as jnp
from jax import lax
from jax.experimental import pallas as pl
from jax.experimental.pallas import tpu as pltpu
from jax.sharding import PartitionSpec as P

D = 2
GROUP = ("tile", "head")
BF = jnp.bfloat16
F32 = jnp.float32
VMEM = pl.BlockSpec(memory_space=pltpu.VMEM)
HBM = pl.BlockSpec(memory_space=pltpu.HBM)
KEPT = 0.90625
REACH = (4, 3, 2)


def params(limit=24 << 20):
    return pltpu.CompilerParams(vmem_limit_bytes=limit)


def in_hbm(*arrays):
    return [pltpu.with_memory_space_constraint(a, pltpu.HBM) for a in arrays]


def my_index():
    return lax.axis_index("tile") * lax.axis_size("head") + lax.axis_index("head")


def put_strips(top, bottom, left, right, mate_ref, other_ref):
    t, _, s, _ = top.shape
    per = s // D
    parity = my_index() % 2

    def put(ref, rows, columns, at_end):
        ref[0:t] = rows[...]
        first = columns.shape[1] - D if at_end else 0
        for i in range(s):
            ref[t, i // per, pl.ds((i % per) * D, D), :] = columns[i, first : first + D, :]

    @pl.when(parity == 0)
    def _():
        put(mate_ref, bottom, right, True)
        put(other_ref, top, left, False)

    @pl.when(parity == 1)
    def _():
        put(mate_ref, top, left, False)
        put(other_ref, bottom, right, True)


def strips_kernel(x_ref, mate_ref, other_ref, top, bottom, left, right, sems):
    t, s = x_ref.shape[:2]
    e = left.shape[1]
    copies = [
        pltpu.make_async_copy(x_ref.at[0, :, 0:e], left, sems.at[0]),
        pltpu.make_async_copy(x_ref.at[t - 1, :, s - e : s], right, sems.at[1]),
        pltpu.make_async_copy(x_ref.at[:, 0:D], top, sems.at[2]),
        pltpu.make_async_copy(x_ref.at[:, s - D : s], bottom, sems.at[3]),
    ]
    for copy in copies:
        copy.start()
    for copy in copies:
        copy.wait()
    put_strips(top, bottom, left, right, mate_ref, other_ref)


def make_strips(x):
    t, s, _, c = x.shape
    out = jax.ShapeDtypeStruct((t + 1, D, s, c), BF)
    return pl.pallas_call(
        strips_kernel,
        out_shape=(out, out),
        in_specs=[HBM],
        out_specs=(VMEM,) * 2,
        scratch_shapes=[pltpu.VMEM((t, D, s, c), BF)] * 2
        + [pltpu.VMEM((s, 16, c), BF)] * 2
        + [pltpu.SemaphoreType.DMA((4,))],
        compiler_params=params(),
        name="strips",
    )(*in_hbm(x))


def swap(mate, other):
    size = lax.axis_size(GROUP)
    mates = [(i, i ^ 1) for i in range(size) if i ^ 1 < size]
    others = [(i, j) for i in range(size) for j in [(i + 1 ^ 1) - 1] if 0 <= j < size]
    return lax.ppermute(mate, GROUP, mates), lax.ppermute(other, GROUP, others)


def regions(t, s):
    inner, outer = [], []
    h = s // 2
    for i in range(t):
        first, last = i == 0, i == t - 1
        outer += [(i, 0, 4, 0, s), (i, s - 4, 4, 0, s)]
        for column in (0, h):
            alone = not (first and column == 0) and not (last and column == h)
            (inner if alone else outer).append((i, 4, s - 8, column, h))
    return inner, outer


def fill_own(tiles, src_ref, win_ref):
    s = src_ref.shape[1]
    for i in tiles:
        v = src_ref[i]
        win_ref[0, i, D : D + s, D:] = v[:, : s - D]
        win_ref[1, i, D : D + s] = v
        win_ref[2, i, D : D + s, : s - D] = v[:, D:]


def fill_beside(tiles, beside_ref, src_ref, win_ref):
    t, s, _, c = src_ref.shape
    for i in tiles:
        if i > 0:
            there = beside_ref[i, 0, 0:D].reshape(1, D, c)
            win_ref[0, i, D : D + s, :D] = src_ref[i - 1, :, s - D :] * there
        if i < t - 1:
            there = beside_ref[i, 1, 0:D].reshape(1, D, c)
            win_ref[2, i, D : D + s, s - D :] = src_ref[i + 1, :, :D] * there


def fill_border(beside_ref, mask_ref, mate_ref, other_ref, win_ref, both_ref):
    t, s, c = win_ref.shape[1], win_ref.shape[3], win_ref.shape[4]
    parity = my_index() % 2
    both_ref[0] = mate_ref[0 : t + 1]
    both_ref[1] = other_ref[0 : t + 1]
    prev_ref, next_ref = both_ref.at[1 - parity], both_ref.at[parity]

    def low(i):
        return prev_ref[t + i] if i < 0 else win_ref[1, i, s : s + D]

    def high(i):
        return next_ref[i - t] if i >= t else win_ref[1, i, D : 2 * D]

    per = s // D
    has_left = beside_ref[0, 0, 0:D]
    has_right = beside_ref[t - 1, 1, 0:D]
    for r in range(s):
        at = pl.ds((r % per) * D, D)
        win_ref[0, 0, D + r, :D] = prev_ref[t, r // per, at, :] * has_left
        win_ref[2, t - 1, D + r, s - D :] = next_ref[t, r // per, at, :] * has_right

    def pick(strip, i, side, kind, columns):
        total = None
        for step in range(1, REACH[kind] + 1):
            rows = strip(i - step if side == 0 else i + step)[:, columns]
            n = rows.shape[1] // 16
            mask = mask_ref[i, side, sum(REACH[:kind]) + step - 1]
            term = rows.reshape(D, n, 16, c) * mask.reshape(1, 1, 16, c)
            total = term if total is None else total + term
        return total.reshape(D, n * 16, c)

    for i in range(t):
        for side, strip, row in ((0, low, 0), (1, high, D + s)):
            rows = slice(row, row + D)
            middle = pick(strip, i, side, 1, slice(0, s))
            left = pick(strip, i, side, 2 * side, slice(s - 16, s))
            right = pick(strip, i, side, 2 - 2 * side, slice(0, 16))
            win_ref[0, i, rows, D:] = middle[:, : s - D]
            win_ref[0, i, rows, :D] = left[:, 16 - D :]
            win_ref[1, i, rows] = middle
            win_ref[2, i, rows, : s - D] = middle[:, D:]
            win_ref[2, i, rows, s - D :] = right[:, :D]


def first_part(places, win_ref, w_ref, bias, u_ref):
    c = w_ref.shape[1] // 2
    pieces = []
    for m in range(4):
        for b in range(3):
            rows = [
                win_ref[b, i, r + D * m : r + D * m + D, q : q + n].reshape(D * n, c)
                for i, row, count, q, n in places
                for r in range(row, row + count, 2 * D)
            ]
            pieces.append(jnp.concatenate(rows, 0))
    both = jnp.dot(jnp.concatenate(pieces, 1), w_ref[...], preferred_element_type=F32)
    total = jnp.zeros((16, c), F32)
    for half in range(2):
        pre = both[:, half * c : (half + 1) * c] + bias
        sig = 0.5 + 0.5 * jnp.tanh(0.5 * pre)
        silu = pre * sig
        total = total + jnp.sum(silu.reshape(-1, 16, c), 0)
        kept = (KEPT * (sig + silu * (1.0 - sig))).astype(BF)
        at = 0
        for i, row, count, q, n in places:
            for r in range(row + D * half, row + count, 2 * D):
                u_ref[i, r : r + D, q : q + n] = kept[at : at + D * n].reshape(D, n, c)
                at += D * n
    return total


def second_part(places, win_ref, w_ref, v_ref):
    c = w_ref.shape[1] // 2
    pieces = []
    for a in range(3):
        for b in range(3):
            rows = [
                win_ref[b, i, r + D * a : r + D * a + count, q : q + n].reshape(count * n, c)
                for i, r, count, q, n in places
            ]
            pieces.append(jnp.concatenate(rows, 0))
    both = jnp.dot(jnp.concatenate(pieces, 1), w_ref[...], preferred_element_type=F32)
    out = both[:, :c] + both[:, c:]
    at = 0
    for i, r, count, q, n in places:
        v_ref[i, r : r + count, q : q + n] = out[at : at + count * n].reshape(count, n, c)
        at += count * n


def inner_kernel(
    x_hbm, w_hbm, near_hbm, bias_hbm, head_hbm, label_hbm,
    u_ref, win_ref, first_ref, second_ref, sum_ref, small_ref, beside_ref, mask_ref,
    x_ref, w_ref, bias_ref, head_ref, near_ref, label_ref, sems,
):
    t, s, _, c = x_ref.shape
    moves = [
        (x_hbm, x_ref), (w_hbm, w_ref), (head_hbm, head_ref), (bias_hbm, bias_ref),
        (near_hbm, near_ref), (label_hbm, label_ref),
    ]
    copies = [pltpu.make_async_copy(a, b, sems.at[i]) for i, (a, b) in enumerate(moves)]
    for copy in copies:
        copy.start()
    for copy in copies[1:]:
        copy.wait()
    small_ref[0:1] = head_ref[...]
    small_ref[1:2] = bias_ref[...]
    small_ref[2:3] = jnp.full((1, c), label_ref[0], jnp.int32).astype(F32)
    start = my_index() * t

    def flag(yes):
        return jnp.full((16, c), jnp.where(yes, 1.0, 0.0), F32).astype(BF)

    for i in range(t):
        beside_ref[i, 0] = flag(near_ref[i, 3] >= 0)
        beside_ref[i, 1] = flag(near_ref[i, 4] >= 0)
        for side in range(2):
            at = 0
            for kind in range(3):
                k = kind if side == 0 else 7 - kind
                for step in range(1, REACH[kind] + 1):
                    there = start + (i - step if side == 0 else i + step)
                    mask_ref[i, side, at] = flag((near_ref[i, k] == there) & (there >= 0))
                    at += 1
    blank = jnp.zeros((c, c), BF)
    head = head_ref[...] * (1.0 / KEPT)
    for b in range(3):
        for m in range(4):
            rows = pl.ds((m * 3 + b) * c, c)
            for half in range(2):
                a = m - half
                first_ref[rows, pl.ds(half * c, c)] = w_ref[a, b] if 0 <= a < 3 else blank
        for a in range(3):
            rows = pl.ds((a * 3 + b) * c, c)
            turned = (w_ref[2 - a, 2 - b].astype(F32) * head).T
            upper = turned.astype(BF)
            second_ref[rows, 0:c] = upper
            second_ref[rows, c : 2 * c] = (turned - upper.astype(F32)).astype(BF)
    copies[0].wait()
    fill_own(range(t), x_ref, win_ref)
    fill_beside(range(t), beside_ref, x_ref, win_ref)
    sum_ref[...] = first_part(regions(t, s)[0], win_ref, first_ref, bias_ref[...], u_ref)


def inner_stage(x, w, near, bias, head, label):
    t, s, _, c = x.shape
    return pl.pallas_call(
        inner_kernel,
        out_shape=(
            jax.ShapeDtypeStruct(x.shape, BF),
            jax.ShapeDtypeStruct((3, t, s + 2 * D, s, c), BF),
            jax.ShapeDtypeStruct((12 * c, 2 * c), BF),
            jax.ShapeDtypeStruct((9 * c, 2 * c), BF),
            jax.ShapeDtypeStruct((16, c), F32),
            jax.ShapeDtypeStruct((3, c), F32),
            jax.ShapeDtypeStruct((t, 2, 16, c), BF),
            jax.ShapeDtypeStruct((t, 2, sum(REACH), 16, c), BF),
        ),
        in_specs=[HBM] * 6,
        out_specs=(VMEM,) * 8,
        scratch_shapes=[
            pltpu.VMEM(x.shape, BF),
            pltpu.VMEM(w.shape, BF),
            pltpu.VMEM((1, c), F32),
            pltpu.VMEM((1, c), F32),
            pltpu.SMEM(near.shape, jnp.int32),
            pltpu.SMEM((1,), jnp.int32),
            pltpu.SemaphoreType.DMA((6,)),
        ],
        compiler_params=params(),
        cost_estimate=pl.CostEstimate(
            flops=9 * t * s * s * c * c, bytes_accessed=6 << 20, transcendentals=t * s * s * c // 2
        ),
        name="inner",
    )(*in_hbm(x, w, near, bias, head), label)


def outer_kernel(
    mate_ref, other_ref, w_ref, small_ref, beside_ref, mask_ref, part_ref, u_in, win_in,
    u_ref, win_ref, to_mate_ref, to_other_ref, sum_ref, both_ref,
):
    del u_in, win_in
    t, s, _, c = u_ref.shape
    fill_border(beside_ref, mask_ref, mate_ref, other_ref, win_ref, both_ref)
    total = part_ref[...] + first_part(
        regions(t, s)[1], win_ref, w_ref, small_ref[1:2], u_ref
    )
    total = total * small_ref[0:1]
    sum_ref[...] = total
    put_strips(
        u_ref.at[:, 0:D], u_ref.at[:, s - D : s],
        u_ref.at[0, :, 0:16], u_ref.at[t - 1, :, s - 16 : s], to_mate_ref, to_other_ref,
    )
    upper = total.astype(BF)
    rest = total - upper.astype(F32)
    middle = rest.astype(BF)
    to_mate_ref[t + 1, 0, 0:16] = upper
    to_mate_ref[t + 1, 0, 16:32] = middle
    to_mate_ref[t + 1, 1, 0:16] = (rest - middle.astype(F32)).astype(BF)
    to_mate_ref[t + 1, 1, 16:32] = jnp.zeros((16, c), BF)


def outer_stage(mate, other, w, small, beside, mask, part, u, win):
    t, s, _, c = u.shape
    return pl.pallas_call(
        outer_kernel,
        out_shape=(
            jax.ShapeDtypeStruct(u.shape, BF),
            jax.ShapeDtypeStruct(win.shape, BF),
            jax.ShapeDtypeStruct((t + 2, D, s, c), BF),
            jax.ShapeDtypeStruct((t + 1, D, s, c), BF),
            jax.ShapeDtypeStruct((16, c), F32),
        ),
        in_specs=[VMEM] * 9,
        out_specs=(VMEM,) * 5,
        input_output_aliases={7: 0, 8: 1},
        scratch_shapes=[pltpu.VMEM((2, t + 1, D, s, c), BF)],
        compiler_params=params(),
        cost_estimate=pl.CostEstimate(
            flops=9 * t * s * s * c * c, bytes_accessed=4 << 20, transcendentals=t * s * s * c // 2
        ),
        name="outer",
    )(mate, other, w, small, beside, mask, part, u, win)


def back_inner_kernel(tiles, u_ref, w_ref, beside_ref, *refs):
    win_ref, v_ref = refs[-2:]
    t, s = u_ref.shape[:2]
    fill_own(tiles, u_ref, win_ref)
    fill_beside(tiles, beside_ref, u_ref, win_ref)
    places = [p for p in regions(t, s)[0] if p[0] in tiles]
    second_part(places, win_ref, w_ref, v_ref)


def back_inner(tiles, u, w, beside, held=()):
    t, s, _, c = u.shape
    return pl.pallas_call(
        functools.partial(back_inner_kernel, tiles),
        out_shape=(
            jax.ShapeDtypeStruct((3, t, s + 2 * D, s, c), BF),
            jax.ShapeDtypeStruct(u.shape, F32),
        ),
        in_specs=[VMEM] * (3 + len(held)),
        out_specs=(VMEM, VMEM),
        input_output_aliases={3: 0, 4: 1} if held else {},
        compiler_params=params(),
        cost_estimate=pl.CostEstimate(
            flops=5 * t * s * s * c * c, bytes_accessed=2 << 20, transcendentals=0
        ),
        name="back_inner",
    )(u, w, beside, *held)


def back_outer_kernel(mate_ref, other_ref, w_ref, beside_ref, mask_ref, win_in, v_in, win_ref, v_ref, both_ref):
    del win_in, v_in
    t, s = v_ref.shape[:2]
    fill_border(beside_ref, mask_ref, mate_ref, other_ref, win_ref, both_ref)
    second_part(regions(t, s)[1], win_ref, w_ref, v_ref)


def back_outer(mate, other, w, beside, mask, win, v):
    t, s, _, c = v.shape
    return pl.pallas_call(
        back_outer_kernel,
        out_shape=(
            jax.ShapeDtypeStruct(win.shape, BF),
            jax.ShapeDtypeStruct(v.shape, F32),
        ),
        in_specs=[VMEM] * 7,
        out_specs=(VMEM, VMEM),
        input_output_aliases={5: 0, 6: 1},
        scratch_shapes=[pltpu.VMEM((2, t + 1, D, s, c), BF)],
        compiler_params=params(),
        cost_estimate=pl.CostEstimate(
            flops=8 * t * s * s * c * c, bytes_accessed=2 << 20, transcendentals=0
        ),
        name="back_outer",
    )(mate, other, w, beside, mask, win, v)[1]


def scale_kernel(count, small_ref, mine_ref, theirs_ref, v_ref, o_ref, stage_ref, sems):
    score = jnp.sum(mine_ref[...] + theirs_ref[...], axis=(0, 1), keepdims=True) / count
    slope = jax.nn.sigmoid(score) - small_ref[2:3, 0:1] / 100.0
    t, s = v_ref.shape[:2]
    copies = []
    for i in range(t):
        for h in range(2):
            rows = pl.ds(h * s // 2, s // 2)
            stage_ref[i, rows] = v_ref[i, rows] * slope.reshape(1, 1, 1)
            copy = pltpu.make_async_copy(stage_ref.at[i, rows], o_ref.at[i, rows], sems.at[i, h])
            copy.start()
            copies.append(copy)
    for copy in copies:
        copy.wait()


def scale(small, mine, theirs, v, count):
    return pl.pallas_call(
        functools.partial(scale_kernel, count),
        out_shape=jax.ShapeDtypeStruct(v.shape, F32),
        in_specs=[VMEM] * 4,
        out_specs=HBM,
        scratch_shapes=[pltpu.VMEM(v.shape, F32), pltpu.SemaphoreType.DMA((v.shape[0], 2))],
        compiler_params=params(),
        name="scale",
    )(small, mine, theirs, v)


def body(tissue_tiles, neighbours, conv_weight, conv_bias, head_weight, slide_label):
    t, s, _, c = tissue_tiles.shape
    size = lax.axis_size(GROUP)
    mate, other = swap(*make_strips(tissue_tiles))
    u, win, w_first, w_second, part, small, beside, mask = inner_stage(
        tissue_tiles, conv_weight, neighbours, conv_bias.reshape(1, c), head_weight.reshape(1, c),
        slide_label,
    )
    u, _, mate, other, mine = outer_stage(
        mate, other, w_first, small, beside, mask, part, u, win
    )
    mate, other = swap(mate, other)
    got = mate[t + 1].astype(F32)
    theirs = got[0, 0:16] + got[0, 16:32] + got[1, 0:16]
    if size & (size - 1):
        mine, theirs = lax.psum(mine, GROUP), jnp.zeros_like(mine)
    step = 2
    while step < size and not size & (size - 1):
        mine = mine + theirs
        theirs = lax.ppermute(mine, GROUP, [(i, i ^ step) for i in range(size)])
        step *= 2
    held = back_inner(tuple(range(1, t - 1)), u, w_second, beside)
    held = back_inner((0, t - 1), u, w_second, beside, held)
    v = back_outer(mate, other, w_second, beside, mask, *held)
    return scale(small, mine, theirs, v, float(t * size * s * s * c))


def solution(mesh):
    return jax.shard_map(
        body,
        mesh=mesh,
        in_specs=(
            P(("groups", "tile", "head"), None, None, None),
            P(("groups", "tile", "head"), None),
            P(),
            P(),
            P(),
            P("groups"),
        ),
        out_specs=P(("groups", "tile", "head"), None, None, None),
        check_vma=False,
    )
```

```python
import functools

import jax
import jax.numpy as jnp
from jax import lax
from jax.experimental import pallas as pl
from jax.experimental.pallas import tpu as pltpu
from jax.sharding import PartitionSpec as P

D = 2
GROUP = ("tile", "head")
BF = jnp.bfloat16
F32 = jnp.float32
VMEM = pl.BlockSpec(memory_space=pltpu.VMEM)
SMEM = pl.BlockSpec(memory_space=pltpu.SMEM)
HBM = pl.BlockSpec(memory_space=pltpu.HBM)
KEPT = 0.90625
REACH = (4, 3, 2)


def params(limit=24 << 20):
    return pltpu.CompilerParams(vmem_limit_bytes=limit)


def in_hbm(*arrays):
    return [pltpu.with_memory_space_constraint(a, pltpu.HBM) for a in arrays]


def my_index():
    return lax.axis_index("tile") * lax.axis_size("head") + lax.axis_index("head")


def put_strips(top, bottom, left, right, mate_ref, other_ref):
    t, _, s, _ = top.shape
    per = s // D
    parity = my_index() % 2

    def put(ref, rows, columns, below):
        far, near = (0, t - 1) if below else (t - 1, 0)
        for i in range(t):
            if i != far:
                ref[i] = rows[i]
        first = columns.shape[1] - D if below else 0
        shared = range(s - D, s) if below else range(D)
        for i in range(s):
            at = pl.ds((i % per) * D, D)
            if i in shared:
                edge = s - D if below else 0
                ref[far, i // per, at, :] = rows[far, i - shared[0], edge : edge + D, :]
            else:
                ref[far, i // per, at, :] = columns[i, first : first + D, :]

    @pl.when(parity == 0)
    def _():
        put(mate_ref, bottom, right, True)
        put(other_ref, top, left, False)

    @pl.when(parity == 1)
    def _():
        put(mate_ref, top, left, False)
        put(other_ref, bottom, right, True)


def strips_kernel(x_ref, mate_ref, other_ref, top, bottom, left, right, sems):
    t, s = x_ref.shape[:2]
    e = left.shape[1]
    copies = [
        pltpu.make_async_copy(x_ref.at[0, :, 0:e], left, sems.at[0]),
        pltpu.make_async_copy(x_ref.at[t - 1, :, s - e : s], right, sems.at[1]),
        pltpu.make_async_copy(x_ref.at[:, 0:D], top, sems.at[2]),
        pltpu.make_async_copy(x_ref.at[:, s - D : s], bottom, sems.at[3]),
    ]
    for copy in copies:
        copy.start()
    for copy in copies:
        copy.wait()
    put_strips(top, bottom, left, right, mate_ref, other_ref)


def make_strips(x):
    t, s, _, c = x.shape
    out = jax.ShapeDtypeStruct((t, D, s, c), BF)
    return pl.pallas_call(
        strips_kernel,
        out_shape=(out, out),
        in_specs=[HBM],
        out_specs=(VMEM,) * 2,
        scratch_shapes=[pltpu.VMEM((t, D, s, c), BF)] * 2
        + [pltpu.VMEM((s, 16, c), BF)] * 2
        + [pltpu.SemaphoreType.DMA((4,))],
        compiler_params=params(),
        name="strips",
    )(*in_hbm(x))


def swap(mate, other):
    size = lax.axis_size(GROUP)
    mates = [(i, i ^ 1) for i in range(size) if i ^ 1 < size]
    others = [(i, j) for i in range(size) for j in [(i + 1 ^ 1) - 1] if 0 <= j < size]
    return (
        None if mate is None else lax.ppermute(mate, GROUP, mates),
        None if other is None else lax.ppermute(other, GROUP, others),
    )


def regions(t, s):
    inner, outer = [], []
    h = s // 2
    for i in range(t):
        first, last = i == 0, i == t - 1
        outer += [(i, 0, 4, 0, s), (i, s - 4, 4, 0, s)]
        for column in (0, h):
            alone = not (first and column == 0) and not (last and column == h)
            (inner if alone else outer).append((i, 4, s - 8, column, h))
    return inner, outer


def fill_own(tiles, src_ref, win_ref):
    s = src_ref.shape[1]
    for i in tiles:
        v = src_ref[i]
        win_ref[0, i, D : D + s, D:] = v[:, : s - D]
        win_ref[1, i, D : D + s] = v
        win_ref[2, i, D : D + s, : s - D] = v[:, D:]


def fill_beside(tiles, beside_ref, src_ref, win_ref):
    t, s, _, c = src_ref.shape
    for i in tiles:
        if i > 0:
            there = beside_ref[i, 0, 0:D].reshape(1, D, c)
            win_ref[0, i, D : D + s, :D] = src_ref[i - 1, :, s - D :] * there
        if i < t - 1:
            there = beside_ref[i, 1, 0:D].reshape(1, D, c)
            win_ref[2, i, D : D + s, s - D :] = src_ref[i + 1, :, :D] * there


def fill_border(beside_ref, mask_ref, mate_ref, other_ref, win_ref, both_ref, corner_ref):
    t, s, c = win_ref.shape[1], win_ref.shape[3], win_ref.shape[4]
    parity = my_index() % 2
    both_ref[0] = mate_ref[0:t]
    both_ref[1] = other_ref[0:t]
    prev_ref, next_ref = both_ref.at[1 - parity], both_ref.at[parity]
    per = s // D
    corner_ref[...] = jnp.zeros(corner_ref.shape, BF)
    for r in range(D):
        at = pl.ds((per - D + r) * D, D)
        corner_ref[0, r, 16 - D :] = prev_ref[0, D - 1, at, :]
        corner_ref[1, r, :D] = next_ref[t - 1, 0, pl.ds(r * D, D), :]

    def low(i, columns):
        if i == -t:
            return corner_ref[0]
        return prev_ref[t + i, :, columns] if i < 0 else win_ref[1, i, s : s + D, columns]

    def high(i, columns):
        if i == 2 * t - 1:
            return corner_ref[1]
        return next_ref[i - t, :, columns] if i >= t else win_ref[1, i, D : 2 * D, columns]

    has_left = beside_ref[0, 0, 0:D]
    has_right = beside_ref[t - 1, 1, 0:D]
    for r in range(s):
        at = pl.ds((r % per) * D, D)
        if r < s - D:
            pixels = prev_ref[0, r // per, at, :]
        else:
            pixels = prev_ref[t - 1, r - s + D, s - D :, :]
        win_ref[0, 0, D + r, :D] = pixels * has_left
        if r >= D:
            pixels = next_ref[t - 1, r // per, at, :]
        else:
            pixels = next_ref[0, r, :D, :]
        win_ref[2, t - 1, D + r, s - D :] = pixels * has_right

    def pick(strip, i, side, kind, columns):
        total = None
        for step in range(1, REACH[kind] + 1):
            rows = strip(i - step if side == 0 else i + step, columns)
            n = rows.shape[1] // 16
            mask = mask_ref[i, side, sum(REACH[:kind]) + step - 1]
            term = rows.reshape(D, n, 16, c) * mask.reshape(1, 1, 16, c)
            total = term if total is None else total + term
        return total.reshape(D, n * 16, c)

    for i in range(t):
        for side, strip, row in ((0, low, 0), (1, high, D + s)):
            rows = slice(row, row + D)
            middle = pick(strip, i, side, 1, slice(0, s))
            left = pick(strip, i, side, 2 * side, slice(s - 16, s))
            right = pick(strip, i, side, 2 - 2 * side, slice(0, 16))
            win_ref[0, i, rows, D:] = middle[:, : s - D]
            win_ref[0, i, rows, :D] = left[:, 16 - D :]
            win_ref[1, i, rows] = middle
            win_ref[2, i, rows, : s - D] = middle[:, D:]
            win_ref[2, i, rows, s - D :] = right[:, :D]


def first_part(places, win_ref, w_ref, bias, u_ref):
    c = w_ref.shape[1] // 2
    pieces = []
    for m in range(4):
        for b in range(3):
            rows = [
                win_ref[b, i, r + D * m : r + D * m + D, q : q + n].reshape(D * n, c)
                for i, row, count, q, n in places
                for r in range(row, row + count, 2 * D)
            ]
            pieces.append(jnp.concatenate(rows, 0))
    both = jnp.dot(jnp.concatenate(pieces, 1), w_ref[...], preferred_element_type=F32)
    total = jnp.zeros((16, c), F32)
    for half in range(2):
        pre = both[:, half * c : (half + 1) * c] + bias
        sig = 0.5 + 0.5 * jnp.tanh(0.5 * pre)
        silu = pre * sig
        total = total + jnp.sum(silu.reshape(-1, 16, c), 0)
        kept = (KEPT * (sig + silu * (1.0 - sig))).astype(BF)
        at = 0
        for i, row, count, q, n in places:
            for r in range(row + D * half, row + count, 2 * D):
                u_ref[i, r : r + D, q : q + n] = kept[at : at + D * n].reshape(D, n, c)
                at += D * n
    return total


def second_part(places, win_ref, w_ref, v_ref):
    c = w_ref.shape[1] // 2
    pieces = []
    for a in range(3):
        for b in range(3):
            rows = [
                win_ref[b, i, r + D * a : r + D * a + count, q : q + n].reshape(count * n, c)
                for i, r, count, q, n in places
            ]
            pieces.append(jnp.concatenate(rows, 0))
    both = jnp.dot(jnp.concatenate(pieces, 1), w_ref[...], preferred_element_type=F32)
    out = both[:, :c] + both[:, c:]
    at = 0
    for i, r, count, q, n in places:
        v_ref[i, r : r + count, q : q + n] = out[at : at + count * n].reshape(count, n, c)
        at += count * n


def inner_kernel(
    x_hbm, w_hbm, near_hbm, bias_hbm, head_hbm,
    u_ref, win_ref, first_ref, sum_ref, small_ref, beside_ref, mask_ref,
    x_ref, w_ref, bias_ref, head_ref, near_ref, sems,
):
    t, s, _, c = x_ref.shape
    moves = [
        (x_hbm, x_ref), (w_hbm, w_ref), (head_hbm, head_ref), (bias_hbm, bias_ref),
        (near_hbm, near_ref),
    ]
    copies = [pltpu.make_async_copy(a, b, sems.at[i]) for i, (a, b) in enumerate(moves)]
    for copy in copies:
        copy.start()
    for copy in copies[1:]:
        copy.wait()
    small_ref[0:1] = head_ref[...]
    small_ref[1:2] = bias_ref[...]
    start = my_index() * t

    def flag(yes):
        return jnp.full((16, c), jnp.where(yes, 1.0, 0.0), F32).astype(BF)

    for i in range(t):
        beside_ref[i, 0] = flag(near_ref[i, 3] >= 0)
        beside_ref[i, 1] = flag(near_ref[i, 4] >= 0)
        for side in range(2):
            at = 0
            for kind in range(3):
                k = kind if side == 0 else 7 - kind
                for step in range(1, REACH[kind] + 1):
                    there = start + (i - step if side == 0 else i + step)
                    mask_ref[i, side, at] = flag((near_ref[i, k] == there) & (there >= 0))
                    at += 1
    blank = jnp.zeros((c, c), BF)
    for b in range(3):
        for m in range(4):
            rows = pl.ds((m * 3 + b) * c, c)
            for half in range(2):
                a = m - half
                first_ref[rows, pl.ds(half * c, c)] = w_ref[a, b] if 0 <= a < 3 else blank
    copies[0].wait()
    fill_own(range(t), x_ref, win_ref)
    fill_beside(range(t), beside_ref, x_ref, win_ref)
    sum_ref[...] = first_part(regions(t, s)[0], win_ref, first_ref, bias_ref[...], u_ref)


def inner_stage(x, w, near, bias, head):
    t, s, _, c = x.shape
    return pl.pallas_call(
        inner_kernel,
        out_shape=(
            jax.ShapeDtypeStruct(x.shape, BF),
            jax.ShapeDtypeStruct((3, t, s + 2 * D, s, c), BF),
            jax.ShapeDtypeStruct((12 * c, 2 * c), BF),
            jax.ShapeDtypeStruct((16, c), F32),
            jax.ShapeDtypeStruct((2, c), F32),
            jax.ShapeDtypeStruct((t, 2, 16, c), BF),
            jax.ShapeDtypeStruct((t, 2, sum(REACH), 16, c), BF),
        ),
        in_specs=[HBM] * 5,
        out_specs=(VMEM,) * 7,
        scratch_shapes=[
            pltpu.VMEM(x.shape, BF),
            pltpu.VMEM(w.shape, BF),
            pltpu.VMEM((1, c), F32),
            pltpu.VMEM((1, c), F32),
            pltpu.SMEM(near.shape, jnp.int32),
            pltpu.SemaphoreType.DMA((5,)),
        ],
        compiler_params=params(),
        cost_estimate=pl.CostEstimate(
            flops=9 * t * s * s * c * c, bytes_accessed=6 << 20, transcendentals=t * s * s * c // 2
        ),
        name="inner",
    )(*in_hbm(x, w, near, bias, head))


def outer_kernel(
    mate_ref, other_ref, w_ref, small_ref, beside_ref, mask_ref, part_ref, u_in, win_in,
    u_ref, win_ref, to_mate_ref, to_other_ref, sum_ref, both_ref, corner_ref,
):
    del u_in, win_in
    t, s, _, c = u_ref.shape
    fill_border(beside_ref, mask_ref, mate_ref, other_ref, win_ref, both_ref, corner_ref)
    total = part_ref[...] + first_part(
        regions(t, s)[1], win_ref, w_ref, small_ref[1:2], u_ref
    )
    total = total * small_ref[0:1]
    sum_ref[...] = total
    put_strips(
        u_ref.at[:, 0:D], u_ref.at[:, s - D : s],
        u_ref.at[0, :, 0:16], u_ref.at[t - 1, :, s - 16 : s], to_mate_ref, to_other_ref,
    )
    upper = total.astype(BF)
    rest = total - upper.astype(F32)
    middle = rest.astype(BF)
    to_mate_ref[t, 0, 0:16] = upper
    to_mate_ref[t, 0, 16:32] = middle
    to_mate_ref[t, 1, 0:16] = (rest - middle.astype(F32)).astype(BF)
    to_mate_ref[t, 1, 16:32] = jnp.zeros((16, c), BF)


def outer_stage(mate, other, w, small, beside, mask, part, u, win):
    t, s, _, c = u.shape
    return pl.pallas_call(
        outer_kernel,
        out_shape=(
            jax.ShapeDtypeStruct(u.shape, BF),
            jax.ShapeDtypeStruct(win.shape, BF),
            jax.ShapeDtypeStruct((t + 1, D, s, c), BF),
            jax.ShapeDtypeStruct((t, D, s, c), BF),
            jax.ShapeDtypeStruct((16, c), F32),
        ),
        in_specs=[VMEM] * 9,
        out_specs=(VMEM,) * 5,
        input_output_aliases={7: 0, 8: 1},
        scratch_shapes=[pltpu.VMEM((2, t, D, s, c), BF), pltpu.VMEM((2, D, 16, c), BF)],
        compiler_params=params(),
        cost_estimate=pl.CostEstimate(
            flops=9 * t * s * s * c * c, bytes_accessed=4 << 20, transcendentals=t * s * s * c // 2
        ),
        name="outer",
    )(mate, other, w, small, beside, mask, part, u, win)


def turn(first_ref, small_ref, second_ref):
    c = first_ref.shape[1] // 2
    head = small_ref[0:1] * (1.0 / KEPT)
    for a in range(3):
        for b in range(3):
            rows = pl.ds((a * 3 + b) * c, c)
            weight = first_ref[pl.ds(((2 - a) * 3 + 2 - b) * c, c), 0:c]
            turned = (weight.astype(F32) * head).T
            upper = turned.astype(BF)
            second_ref[rows, 0:c] = upper
            second_ref[rows, c : 2 * c] = (turned - upper.astype(F32)).astype(BF)


def back_tiles(tiles, u_ref, w_ref, beside_ref, win_ref, v_ref):
    t, s = u_ref.shape[:2]
    fill_own(tiles, u_ref, win_ref)
    fill_beside(tiles, beside_ref, u_ref, win_ref)
    places = [p for p in regions(t, s)[0] if p[0] in tiles]
    second_part(places, win_ref, w_ref, v_ref)


def back_inner_kernel(
    u_ref, first_ref, small_ref, beside_ref, label_ref, win_ref, v_ref, w_ref, row_ref
):
    row_ref[...] = jnp.full(row_ref.shape, label_ref[0], jnp.int32).astype(F32)
    turn(first_ref, small_ref, w_ref)
    back_tiles(range(u_ref.shape[0]), u_ref, w_ref, beside_ref, win_ref, v_ref)


def back_inner(u, first, small, beside, label):
    t, s, _, c = u.shape
    return pl.pallas_call(
        back_inner_kernel,
        out_shape=(
            jax.ShapeDtypeStruct((3, t, s + 2 * D, s, c), BF),
            jax.ShapeDtypeStruct(u.shape, F32),
            jax.ShapeDtypeStruct((9 * c, 2 * c), BF),
            jax.ShapeDtypeStruct((8, c), F32),
        ),
        in_specs=[VMEM] * 4 + [SMEM],
        out_specs=(VMEM,) * 4,
        compiler_params=params(),
        cost_estimate=pl.CostEstimate(
            flops=16 * t * s * s * c * c, bytes_accessed=8 << 20, transcendentals=0
        ),
        name="back_inner",
    )(u, first, small, beside, label)


def gate_kernel(strip_ref, sum_ref, out_ref):
    del sum_ref
    out_ref[...] = strip_ref[...]


def gate(strip, total):
    return pl.pallas_call(
        gate_kernel,
        out_shape=jax.ShapeDtypeStruct(strip.shape, strip.dtype),
        in_specs=[VMEM, VMEM],
        out_specs=VMEM,
        compiler_params=params(),
        cost_estimate=pl.CostEstimate(flops=1 << 31, bytes_accessed=1 << 20, transcendentals=0),
        name="gate",
    )(strip, total)


def back_outer_kernel(mate_ref, other_ref, w_ref, beside_ref, mask_ref, win_in, v_in, win_ref, v_ref, both_ref, corner_ref):
    del win_in, v_in
    t, s = v_ref.shape[:2]
    fill_border(beside_ref, mask_ref, mate_ref, other_ref, win_ref, both_ref, corner_ref)
    second_part(regions(t, s)[1], win_ref, w_ref, v_ref)


def back_outer(mate, other, w, beside, mask, win, v):
    t, s, _, c = v.shape
    return pl.pallas_call(
        back_outer_kernel,
        out_shape=(
            jax.ShapeDtypeStruct(win.shape, BF),
            jax.ShapeDtypeStruct(v.shape, F32),
        ),
        in_specs=[VMEM] * 7,
        out_specs=(VMEM, VMEM),
        input_output_aliases={5: 0, 6: 1},
        scratch_shapes=[pltpu.VMEM((2, t, D, s, c), BF), pltpu.VMEM((2, D, 16, c), BF)],
        compiler_params=params(),
        cost_estimate=pl.CostEstimate(
            flops=8 * t * s * s * c * c, bytes_accessed=2 << 20, transcendentals=0
        ),
        name="back_outer",
    )(mate, other, w, beside, mask, win, v)[1]


def scale_kernel(count, label_ref, mine_ref, theirs_ref, v_ref, o_ref, stage_ref, sems):
    score = jnp.sum(mine_ref[...] + theirs_ref[...], axis=(0, 1), keepdims=True) / count
    slope = jax.nn.sigmoid(score) - label_ref[0:1, 0:1] / 100.0
    t, s = v_ref.shape[:2]
    copies = []
    for i in range(t):
        for h in range(2):
            rows = pl.ds(h * s // 2, s // 2)
            stage_ref[i, rows] = v_ref[i, rows] * slope.reshape(1, 1, 1)
            copy = pltpu.make_async_copy(stage_ref.at[i, rows], o_ref.at[i, rows], sems.at[i, h])
            copy.start()
            copies.append(copy)
    for copy in copies:
        copy.wait()


def scale(label, mine, theirs, v, count):
    return pl.pallas_call(
        functools.partial(scale_kernel, count),
        out_shape=jax.ShapeDtypeStruct(v.shape, F32),
        in_specs=[VMEM] * 4,
        out_specs=HBM,
        scratch_shapes=[pltpu.VMEM(v.shape, F32), pltpu.SemaphoreType.DMA((v.shape[0], 2))],
        compiler_params=params(),
        name="scale",
    )(label, mine, theirs, v)


def body(tissue_tiles, neighbours, conv_weight, conv_bias, head_weight, slide_label):
    t, s, _, c = tissue_tiles.shape
    size = lax.axis_size(GROUP)
    mate, other = swap(*make_strips(tissue_tiles))
    u, win, w_first, part, small, beside, mask = inner_stage(
        tissue_tiles, conv_weight, neighbours, conv_bias.reshape(1, c), head_weight.reshape(1, c)
    )
    u, _, mate, other, mine = outer_stage(
        mate, other, w_first, small, beside, mask, part, u, win
    )
    mate, _ = swap(mate, None)
    got = mate[t].astype(F32)
    theirs = got[0, 0:16] + got[0, 16:32] + got[1, 0:16]
    if size & (size - 1):
        mine, theirs = lax.psum(mine, GROUP), jnp.zeros_like(mine)
    step = 2
    while step < size and not size & (size - 1):
        mine = mine + theirs
        if step == 2:
            other = gate(other, mine)
        theirs = lax.ppermute(mine, GROUP, [(i, i ^ step) for i in range(size)])
        step *= 2
    _, other = swap(None, other)
    win, v, w_second, label = back_inner(u, w_first, small, beside, slide_label)
    v = back_outer(mate, other, w_second, beside, mask, win, v)
    return scale(label, mine, theirs, v, float(t * size * s * s * c))


def solution(mesh):
    return jax.shard_map(
        body,
        mesh=mesh,
        in_specs=(
            P(("groups", "tile", "head"), None, None, None),
            P(("groups", "tile", "head"), None),
            P(),
            P(),
            P(),
            P("groups"),
        ),
        out_specs=P(("groups", "tile", "head"), None, None, None),
        check_vma=False,
    )
```

```python
import functools

import jax
import jax.numpy as jnp
from jax import lax
from jax.experimental import pallas as pl
from jax.experimental.pallas import tpu as pltpu
from jax.sharding import PartitionSpec as P

D = 2
GROUP = ("tile", "head")
BF = jnp.bfloat16
F32 = jnp.float32
VMEM = pl.BlockSpec(memory_space=pltpu.VMEM)
SMEM = pl.BlockSpec(memory_space=pltpu.SMEM)
HBM = pl.BlockSpec(memory_space=pltpu.HBM)
KEPT = 0.90625
REACH = (4, 3, 2)


def params(limit=24 << 20):
    return pltpu.CompilerParams(vmem_limit_bytes=limit)


def in_hbm(*arrays):
    return [pltpu.with_memory_space_constraint(a, pltpu.HBM) for a in arrays]


def my_index():
    return lax.axis_index("tile") * lax.axis_size("head") + lax.axis_index("head")


def put_strips(top, bottom, left, right, mate_ref, other_ref):
    t, _, s, _ = top.shape
    per = s // D
    parity = my_index() % 2

    def put(ref, rows, columns, below):
        far, near = (0, t - 1) if below else (t - 1, 0)
        for i in range(t):
            if i != far:
                ref[i] = rows[i]
        first = columns.shape[1] - D if below else 0
        shared = range(s - D, s) if below else range(D)
        for i in range(s):
            at = pl.ds((i % per) * D, D)
            if i in shared:
                edge = s - D if below else 0
                ref[far, i // per, at, :] = rows[far, i - shared[0], edge : edge + D, :]
            else:
                ref[far, i // per, at, :] = columns[i, first : first + D, :]

    @pl.when(parity == 0)
    def _():
        put(mate_ref, bottom, right, True)
        put(other_ref, top, left, False)

    @pl.when(parity == 1)
    def _():
        put(mate_ref, top, left, False)
        put(other_ref, bottom, right, True)


def strips_kernel(x_ref, mate_ref, other_ref, top, bottom, left, right, sems):
    t, s = x_ref.shape[:2]
    e = left.shape[1]
    copies = [
        pltpu.make_async_copy(x_ref.at[0, :, 0:e], left, sems.at[0]),
        pltpu.make_async_copy(x_ref.at[t - 1, :, s - e : s], right, sems.at[1]),
        pltpu.make_async_copy(x_ref.at[:, 0:D], top, sems.at[2]),
        pltpu.make_async_copy(x_ref.at[:, s - D : s], bottom, sems.at[3]),
    ]
    for copy in copies:
        copy.start()
    for copy in copies:
        copy.wait()
    put_strips(top, bottom, left, right, mate_ref, other_ref)


def make_strips(x):
    t, s, _, c = x.shape
    out = jax.ShapeDtypeStruct((t, D, s, c), BF)
    return pl.pallas_call(
        strips_kernel,
        out_shape=(out, out),
        in_specs=[HBM],
        out_specs=(VMEM,) * 2,
        scratch_shapes=[pltpu.VMEM((t, D, s, c), BF)] * 2
        + [pltpu.VMEM((s, 16, c), BF)] * 2
        + [pltpu.SemaphoreType.DMA((4,))],
        compiler_params=params(),
        cost_estimate=pl.CostEstimate(flops=1 << 32, bytes_accessed=8 << 20, transcendentals=0),
        name="strips",
    )(*in_hbm(x))


def swap(mate, other):
    size = lax.axis_size(GROUP)
    mates = [(i, i ^ 1) for i in range(size) if i ^ 1 < size]
    others = [(i, j) for i in range(size) for j in [(i + 1 ^ 1) - 1] if 0 <= j < size]
    return (
        None if mate is None else lax.ppermute(mate, GROUP, mates),
        None if other is None else lax.ppermute(other, GROUP, others),
    )


def regions(t, s):
    inner, outer = [], []
    h = s // 2
    for i in range(t):
        first, last = i == 0, i == t - 1
        outer += [(i, 0, 4, 0, s), (i, s - 4, 4, 0, s)]
        for column in (0, h):
            alone = not (first and column == 0) and not (last and column == h)
            (inner if alone else outer).append((i, 4, s - 8, column, h))
    return inner, outer


def fill_own(tiles, src_ref, win_ref):
    s = src_ref.shape[1]
    for i in tiles:
        v = src_ref[i]
        win_ref[0, i, D : D + s, D:] = v[:, : s - D]
        win_ref[1, i, D : D + s] = v
        win_ref[2, i, D : D + s, : s - D] = v[:, D:]


def fill_beside(tiles, beside_ref, src_ref, win_ref):
    t, s, _, c = src_ref.shape
    for i in tiles:
        if i > 0:
            there = beside_ref[i, 0, 0:D].reshape(1, D, c)
            win_ref[0, i, D : D + s, :D] = src_ref[i - 1, :, s - D :] * there
        if i < t - 1:
            there = beside_ref[i, 1, 0:D].reshape(1, D, c)
            win_ref[2, i, D : D + s, s - D :] = src_ref[i + 1, :, :D] * there


def fill_side(side, beside_ref, mask_ref, strip_ref, win_ref, corner_ref):
    t, s, c = win_ref.shape[1], win_ref.shape[3], win_ref.shape[4]
    per = s // D
    far, near = (0, t - 1) if side == 0 else (t - 1, 0)
    shared = range(s - D, s) if side == 0 else range(D)
    inside = slice(s - D, s) if side == 0 else slice(0, D)
    corner_ref[...] = jnp.zeros(corner_ref.shape, BF)
    there = beside_ref[0, 0, 0:D] if side == 0 else beside_ref[t - 1, 1, 0:D]
    for r in range(s):
        at = pl.ds((r % per) * D, D)
        pixels = strip_ref[far, r // per, at, :]
        if r in shared:
            edge = slice(16 - D, 16) if side == 0 else slice(0, D)
            corner_ref[r - shared[0], edge] = pixels
            pixels = strip_ref[near, r - shared[0], inside, :]
        if side == 0:
            win_ref[0, 0, D + r, :D] = pixels * there
        else:
            win_ref[2, t - 1, D + r, s - D :] = pixels * there

    def strip(i, columns):
        if i in (-t, 2 * t - 1):
            return corner_ref[...]
        if i < 0:
            return strip_ref[t + i, :, columns]
        if i >= t:
            return strip_ref[i - t, :, columns]
        row = s if side == 0 else D
        return win_ref[1, i, row : row + D, columns]

    def pick(i, kind, columns):
        total = None
        for step in range(1, REACH[kind] + 1):
            rows = strip(i - step if side == 0 else i + step, columns)
            n = rows.shape[1] // 16
            mask = mask_ref[i, side, sum(REACH[:kind]) + step - 1]
            term = rows.reshape(D, n, 16, c) * mask.reshape(1, 1, 16, c)
            total = term if total is None else total + term
        return total.reshape(D, n * 16, c)

    row = 0 if side == 0 else D + s
    for i in range(t):
        rows = slice(row, row + D)
        middle = pick(i, 1, slice(0, s))
        left = pick(i, 2 * side, slice(s - 16, s))
        right = pick(i, 2 - 2 * side, slice(0, 16))
        win_ref[0, i, rows, D:] = middle[:, : s - D]
        win_ref[0, i, rows, :D] = left[:, 16 - D :]
        win_ref[1, i, rows] = middle
        win_ref[2, i, rows, : s - D] = middle[:, D:]
        win_ref[2, i, rows, s - D :] = right[:, :D]


def side_regions(t, s, side, last):
    h = s // 2
    top = [(i, 0, 4, 0, s) for i in range(t)]
    bottom = [(i, s - 4, 4, 0, s) for i in range(t)]
    if side == 0:
        places = top + [(0, 4, s - 8, 0, h)]
        if last:
            return places + [(0, s - 4, 4, 0, h)]
        return places[: t - 1] + [(t - 1, 0, 4, 0, h)] + places[t:]
    places = bottom + [(t - 1, 4, s - 8, h, h)]
    if last:
        return places + [(t - 1, 0, 4, h, h)]
    return [(0, s - 4, 4, h, h)] + places[1:]


def first_part(places, win_ref, w_ref, bias, u_ref):
    c = w_ref.shape[1] // 2
    pieces = []
    for m in range(4):
        for b in range(3):
            rows = [
                win_ref[b, i, r + D * m : r + D * m + D, q : q + n].reshape(D * n, c)
                for i, row, count, q, n in places
                for r in range(row, row + count, 2 * D)
            ]
            pieces.append(jnp.concatenate(rows, 0))
    both = jnp.dot(jnp.concatenate(pieces, 1), w_ref[...], preferred_element_type=F32)
    total = jnp.zeros((16, c), F32)
    for half in range(2):
        pre = both[:, half * c : (half + 1) * c] + bias
        sig = 0.5 + 0.5 * jnp.tanh(0.5 * pre)
        silu = pre * sig
        total = total + jnp.sum(silu.reshape(-1, 16, c), 0)
        kept = (KEPT * (sig + silu * (1.0 - sig))).astype(BF)
        at = 0
        for i, row, count, q, n in places:
            for r in range(row + D * half, row + count, 2 * D):
                u_ref[i, r : r + D, q : q + n] = kept[at : at + D * n].reshape(D, n, c)
                at += D * n
    return total


def second_part(places, win_ref, w_ref, v_ref):
    c = w_ref.shape[1] // 2
    pieces = []
    for a in range(3):
        for b in range(3):
            rows = [
                win_ref[b, i, r + D * a : r + D * a + count, q : q + n].reshape(count * n, c)
                for i, r, count, q, n in places
            ]
            pieces.append(jnp.concatenate(rows, 0))
    both = jnp.dot(jnp.concatenate(pieces, 1), w_ref[...], preferred_element_type=F32)
    out = both[:, :c] + both[:, c:]
    at = 0
    for i, r, count, q, n in places:
        v_ref[i, r : r + count, q : q + n] = out[at : at + count * n].reshape(count, n, c)
        at += count * n


def inner_kernel(
    x_ref, w_ref, bias_ref, near_vmem,
    u_ref, win_ref, first_ref, sum_ref, beside_ref, mask_ref, near_ref, sem,
):
    t, s, _, c = x_ref.shape
    copy = pltpu.make_async_copy(near_vmem, near_ref, sem)
    copy.start()
    blank = jnp.zeros((c, c), BF)
    for b in range(3):
        for m in range(4):
            rows = pl.ds((m * 3 + b) * c, c)
            for half in range(2):
                a = m - half
                first_ref[rows, pl.ds(half * c, c)] = w_ref[a, b] if 0 <= a < 3 else blank
    fill_own(range(t), x_ref, win_ref)
    copy.wait()
    start = my_index() * t

    def flag(yes):
        return jnp.full((16, c), jnp.where(yes, 1.0, 0.0), F32).astype(BF)

    for i in range(t):
        beside_ref[i, 0] = flag(near_ref[i, 3] >= 0)
        beside_ref[i, 1] = flag(near_ref[i, 4] >= 0)
        for side in range(2):
            at = 0
            for kind in range(3):
                k = kind if side == 0 else 7 - kind
                for step in range(1, REACH[kind] + 1):
                    there = start + (i - step if side == 0 else i + step)
                    mask_ref[i, side, at] = flag((near_ref[i, k] == there) & (there >= 0))
                    at += 1
    fill_beside(range(t), beside_ref, x_ref, win_ref)
    sum_ref[...] = first_part(regions(t, s)[0], win_ref, first_ref, bias_ref[...], u_ref)


def inner_stage(x, w, bias, near):
    t, s, _, c = x.shape
    return pl.pallas_call(
        inner_kernel,
        out_shape=(
            jax.ShapeDtypeStruct(x.shape, BF),
            jax.ShapeDtypeStruct((3, t, s + 2 * D, s, c), BF),
            jax.ShapeDtypeStruct((12 * c, 2 * c), BF),
            jax.ShapeDtypeStruct((16, c), F32),
            jax.ShapeDtypeStruct((t, 2, 16, c), BF),
            jax.ShapeDtypeStruct((t, 2, sum(REACH), 16, c), BF),
        ),
        in_specs=[VMEM] * 4,
        out_specs=(VMEM,) * 6,
        scratch_shapes=[pltpu.SMEM(near.shape, jnp.int32), pltpu.SemaphoreType.DMA(())],
        compiler_params=params(),
        cost_estimate=pl.CostEstimate(
            flops=9 * t * s * s * c * c, bytes_accessed=6 << 20, transcendentals=t * s * s * c // 2
        ),
        name="inner",
    )(x, w, bias, near)


def outer_kernel(
    last, strip_ref, w_ref, bias_ref, beside_ref, mask_ref, part_ref, u_in, win_in, u_ref, win_ref, sum_ref, corner_ref,
):
    del u_in, win_in
    t, s = u_ref.shape[:2]
    parity = my_index() % 2

    def run(side):
        fill_side(side, beside_ref, mask_ref, strip_ref, win_ref, corner_ref)
        places = side_regions(t, s, side, last)
        sum_ref[...] = part_ref[...] + first_part(places, win_ref, w_ref, bias_ref[...], u_ref)

    first = parity if last else 1 - parity

    @pl.when(first == 0)
    def _():
        run(0)

    @pl.when(first == 1)
    def _():
        run(1)


def outer_mate_kernel(*refs):
    outer_kernel(False, *refs)


def outer_other_kernel(
    strip_ref, w_ref, bias_ref, head_ref, beside_ref, mask_ref, part_ref, u_in, win_in,
    u_ref, win_ref, to_mate_ref, to_other_ref, sum_ref, corner_ref,
):
    t, s, _, c = u_ref.shape
    outer_kernel(
        True, strip_ref, w_ref, bias_ref, beside_ref, mask_ref, part_ref, u_in, win_in,
        u_ref, win_ref, sum_ref, corner_ref,
    )
    total = sum_ref[...] * head_ref[...]
    sum_ref[...] = total
    put_strips(
        u_ref.at[:, 0:D], u_ref.at[:, s - D : s],
        u_ref.at[0, :, 0:16], u_ref.at[t - 1, :, s - 16 : s], to_mate_ref, to_other_ref,
    )
    upper = total.astype(BF)
    rest = total - upper.astype(F32)
    middle = rest.astype(BF)
    to_mate_ref[t, 0, 0:16] = upper
    to_mate_ref[t, 0, 16:32] = middle
    to_mate_ref[t, 1, 0:16] = (rest - middle.astype(F32)).astype(BF)
    to_mate_ref[t, 1, 16:32] = jnp.zeros((16, c), BF)


def outer_mate(strip, w, bias, beside, mask, part, u, win):
    t, s, _, c = u.shape
    return pl.pallas_call(
        outer_mate_kernel,
        out_shape=(
            jax.ShapeDtypeStruct(u.shape, BF),
            jax.ShapeDtypeStruct(win.shape, BF),
            jax.ShapeDtypeStruct((16, c), F32),
        ),
        in_specs=[VMEM] * 8,
        out_specs=(VMEM,) * 3,
        input_output_aliases={6: 0, 7: 1},
        scratch_shapes=[pltpu.VMEM((D, 16, c), BF)],
        compiler_params=params(),
        cost_estimate=pl.CostEstimate(
            flops=4 * t * s * s * c * c, bytes_accessed=4 << 20, transcendentals=t * s * s * c // 4
        ),
        name="outer_mate",
    )(strip, w, bias, beside, mask, part, u, win)


def outer_other(strip, w, bias, head, beside, mask, part, u, win):
    t, s, _, c = u.shape
    return pl.pallas_call(
        outer_other_kernel,
        out_shape=(
            jax.ShapeDtypeStruct(u.shape, BF),
            jax.ShapeDtypeStruct(win.shape, BF),
            jax.ShapeDtypeStruct((t + 1, D, s, c), BF),
            jax.ShapeDtypeStruct((t, D, s, c), BF),
            jax.ShapeDtypeStruct((16, c), F32),
        ),
        in_specs=[VMEM] * 9,
        out_specs=(VMEM,) * 5,
        input_output_aliases={7: 0, 8: 1},
        scratch_shapes=[pltpu.VMEM((D, 16, c), BF)],
        compiler_params=params(),
        cost_estimate=pl.CostEstimate(
            flops=4 * t * s * s * c * c, bytes_accessed=4 << 20, transcendentals=t * s * s * c // 4
        ),
        name="outer_other",
    )(strip, w, bias, head, beside, mask, part, u, win)


def turn(first_ref, head_ref, second_ref):
    c = first_ref.shape[1] // 2
    head = head_ref[...] * (1.0 / KEPT)
    for a in range(3):
        for b in range(3):
            rows = pl.ds((a * 3 + b) * c, c)
            weight = first_ref[pl.ds(((2 - a) * 3 + 2 - b) * c, c), 0:c]
            turned = (weight.astype(F32) * head).T
            upper = turned.astype(BF)
            second_ref[rows, 0:c] = upper
            second_ref[rows, c : 2 * c] = (turned - upper.astype(F32)).astype(BF)


def back_tiles(tiles, u_ref, w_ref, beside_ref, win_ref, v_ref):
    t, s = u_ref.shape[:2]
    fill_own(tiles, u_ref, win_ref)
    fill_beside(tiles, beside_ref, u_ref, win_ref)
    places = [p for p in regions(t, s)[0] if p[0] in tiles]
    second_part(places, win_ref, w_ref, v_ref)


def turned(first, head):
    c = head.shape[1]
    return pl.pallas_call(
        turn,
        out_shape=jax.ShapeDtypeStruct((9 * c, 2 * c), BF),
        in_specs=[VMEM, VMEM],
        out_specs=VMEM,
        compiler_params=params(),
        cost_estimate=pl.CostEstimate(flops=0, bytes_accessed=1 << 20, transcendentals=0),
        name="turn",
    )(first, head)


def back_inner_kernel(u_ref, w_ref, beside_ref, label_ref, win_ref, v_ref, row_ref):
    row_ref[...] = jnp.full(row_ref.shape, label_ref[0], jnp.int32).astype(F32)
    back_tiles(range(u_ref.shape[0]), u_ref, w_ref, beside_ref, win_ref, v_ref)


def back_inner(u, w, beside, label):
    t, s, _, c = u.shape
    return pl.pallas_call(
        back_inner_kernel,
        out_shape=(
            jax.ShapeDtypeStruct((3, t, s + 2 * D, s, c), BF),
            jax.ShapeDtypeStruct(u.shape, F32),
            jax.ShapeDtypeStruct((8, c), F32),
        ),
        in_specs=[VMEM] * 3 + [SMEM],
        out_specs=(VMEM,) * 3,
        compiler_params=params(),
        cost_estimate=pl.CostEstimate(
            flops=16 * t * s * s * c * c, bytes_accessed=8 << 20, transcendentals=0
        ),
        name="back_inner",
    )(u, w, beside, label)


def gate_kernel(strip_ref, sum_ref, out_ref):
    del sum_ref
    out_ref[...] = strip_ref[...]


def gate(strip, total):
    return pl.pallas_call(
        gate_kernel,
        out_shape=jax.ShapeDtypeStruct(strip.shape, strip.dtype),
        in_specs=[VMEM, VMEM],
        out_specs=VMEM,
        compiler_params=params(),
        cost_estimate=pl.CostEstimate(flops=1 << 31, bytes_accessed=1 << 20, transcendentals=0),
        name="gate",
    )(strip, total)


def back_outer_kernel(mate_ref, other_ref, w_ref, beside_ref, mask_ref, win_in, v_in, win_ref, v_ref, both_ref, corner_ref):
    del win_in, v_in
    t, s = v_ref.shape[:2]
    parity = my_index() % 2
    both_ref[0] = mate_ref[0:t]
    both_ref[1] = other_ref[0:t]
    for side, strip_ref in enumerate((both_ref.at[1 - parity], both_ref.at[parity])):
        fill_side(side, beside_ref, mask_ref, strip_ref, win_ref, corner_ref.at[side])
    second_part(regions(t, s)[1], win_ref, w_ref, v_ref)


def back_outer(mate, other, w, beside, mask, win, v):
    t, s, _, c = v.shape
    return pl.pallas_call(
        back_outer_kernel,
        out_shape=(
            jax.ShapeDtypeStruct(win.shape, BF),
            jax.ShapeDtypeStruct(v.shape, F32),
        ),
        in_specs=[VMEM] * 7,
        out_specs=(VMEM, VMEM),
        input_output_aliases={5: 0, 6: 1},
        scratch_shapes=[pltpu.VMEM((2, t, D, s, c), BF), pltpu.VMEM((2, D, 16, c), BF)],
        compiler_params=params(),
        cost_estimate=pl.CostEstimate(
            flops=8 * t * s * s * c * c, bytes_accessed=2 << 20, transcendentals=0
        ),
        name="back_outer",
    )(mate, other, w, beside, mask, win, v)[1]


def scale_kernel(count, label_ref, mine_ref, theirs_ref, v_ref, o_ref, stage_ref, sems):
    score = jnp.sum(mine_ref[...] + theirs_ref[...], axis=(0, 1), keepdims=True) / count
    slope = jax.nn.sigmoid(score) - label_ref[0:1, 0:1] / 100.0
    t, s = v_ref.shape[:2]
    copies = []
    for i in range(t):
        for h in range(2):
            rows = pl.ds(h * s // 2, s // 2)
            stage_ref[i, rows] = v_ref[i, rows] * slope.reshape(1, 1, 1)
            copy = pltpu.make_async_copy(stage_ref.at[i, rows], o_ref.at[i, rows], sems.at[i, h])
            copy.start()
            copies.append(copy)
    for copy in copies:
        copy.wait()


def scale(label, mine, theirs, v, count):
    return pl.pallas_call(
        functools.partial(scale_kernel, count),
        out_shape=jax.ShapeDtypeStruct(v.shape, F32),
        in_specs=[VMEM] * 4,
        out_specs=HBM,
        scratch_shapes=[pltpu.VMEM(v.shape, F32), pltpu.SemaphoreType.DMA((v.shape[0], 2))],
        compiler_params=params(),
        name="scale",
    )(label, mine, theirs, v)


def body(tissue_tiles, neighbours, conv_weight, conv_bias, head_weight, slide_label):
    t, s, _, c = tissue_tiles.shape
    size = lax.axis_size(GROUP)
    mate, other = swap(*make_strips(tissue_tiles))
    bias, head = conv_bias.reshape(1, c), head_weight.reshape(1, c)
    u, win, w_first, part, beside, mask = inner_stage(tissue_tiles, conv_weight, bias, neighbours)
    u, win, part = outer_mate(mate, w_first, bias, beside, mask, part, u, win)
    u, _, mate, other, mine = outer_other(
        other, w_first, bias, head, beside, mask, part, u, win
    )
    mate, _ = swap(mate, None)
    got = mate[t].astype(F32)
    theirs = got[0, 0:16] + got[0, 16:32] + got[1, 0:16]
    if size & (size - 1):
        mine, theirs = lax.psum(mine, GROUP), jnp.zeros_like(mine)
    step = 2
    while step < size and not size & (size - 1):
        mine = mine + theirs
        if step == 2:
            other = gate(other, mine)
        theirs = lax.ppermute(mine, GROUP, [(i, i ^ step) for i in range(size)])
        step *= 2
    _, other = swap(None, other)
    w_second = turned(w_first, head)
    win, v, label = back_inner(u, w_second, beside, slide_label)
    v = back_outer(mate, other, w_second, beside, mask, win, v)
    return scale(label, mine, theirs, v, float(t * size * s * s * c))


def solution(mesh):
    return jax.shard_map(
        body,
        mesh=mesh,
        in_specs=(
            P(("groups", "tile", "head"), None, None, None),
            P(("groups", "tile", "head"), None),
            P(),
            P(),
            P(),
            P("groups"),
        ),
        out_specs=P(("groups", "tile", "head"), None, None, None),
        check_vma=False,
    )
```
